32 devices in a mesh: groups: 2 (over y), space: 4 (over z), tm: 2 (over x), chan: 2 (over core).
Axes of the slice: x: 2, y: 2, z: 4, core: 2. Of those that a mesh axis runs over, the one named last changes fastest.
Arguments:
- latent: bfloat16 [4, 16, 1024], P(('groups', 'tm'), 'space'), parts along dimension 0, may hold values from -12 to 12
- in_weight: bfloat16 [432, 384], P(None, 'chan'), may hold values from -1.5 to 1.5
- in_bias: float32 [384], P('chan'), may hold values from -1.5 to 1.5
- first_gain: float32 [384], replicated, may hold values from 0.25 to 1.75
- first_weight: bfloat16 [9, 1152, 384], P(None, None, 'chan'), may hold values from -0.0625 to 0.0625
- first_bias: float32 [384], P('chan'), may hold values from -1.5 to 1.5
- second_gain: float32 [384], replicated, may hold values from 0.25 to 1.75
- second_weight: bfloat16 [9, 1152, 384], P(None, None, 'chan'), may hold values from -0.0625 to 0.0625
- second_bias: float32 [384], P('chan'), may hold values from -1.5 to 1.5
- up_weight: bfloat16 [3, 1152, 192], P(None, None, 'chan'), may hold values from -0.109375 to 0.109375
- up_bias: float32 [192], P('chan'), may hold values from -1.5 to 1.5
Outputs:
- decoded: bfloat16 [8, 16, 192, 128], P(('groups', 'tm'), 'space', 'chan'), parts along dimension 0
The draws below stay inside these ranges and needn't reach their ends.
There are 2 independent parts, one for each index of `groups`. The reference program is written for one: setup_inputs(seed, part) draws one part's arguments, and reference() takes and returns one part's arrays. A program takes and returns all parts, laid end to end along the dimension named above; an argument that names none is the same for every part. Nothing has to cross between parts.
All inputs are finite; a program needn't handle non-finite values.
Results may differ from the reference program's by a relative error of at most 0.0058.
Values may be sent and summed in bfloat16 or wider, within the bound.
No kernel may reach another device: no remote copies, remote signals or barrier semaphores. Data moves between devices by JAX's collectives and lax.ppermute only.
A program may use at most 64 MiB of HBM per device.

```python
import math
import jax
import jax.numpy as jnp
from jax import lax

ZC = 16
C = 384
CU = 192
FS = 2
LW = 64
SECTIONS = 2
LH = 8


def draw_latent(key, part):
    first_key, second_key = jax.random.split(key, 2)
    shape = (SECTIONS, FS * LH, LW, ZC)
    values = jnp.clip(jax.random.normal(first_key, shape, jnp.float32), -4.0, 4.0)
    spread = jax.random.uniform(second_key, (SECTIONS, FS * LH, LW, 1), jnp.float32, math.log(0.3), math.log(3.0))
    return (values * jnp.exp(spread)).reshape(SECTIONS, FS * LH, LW * ZC).astype(jnp.bfloat16)


def draw_in_weight(key, part):
    first_key, second_key = jax.random.split(key)
    values = jnp.clip(jax.random.normal(first_key, (27 * ZC, C), jnp.float32), -4.0, 4.0)
    position = jnp.arange(C).astype(jnp.float32) / C
    jitter = jax.random.uniform(second_key, (1, C), jnp.float32, -0.3, 0.3)
    factor = jnp.exp(math.log(0.3) + math.log(10.0) * position + jitter)
    return (values * factor * (27 * ZC) ** (-0.5)).astype(jnp.bfloat16)


def shard_levels(own_key, dims, cuts, least, high):
    def one(dim, parts):
        draws = jax.random.uniform(jax.random.fold_in(jax.random.fold_in(own_key, 6), dim), (parts,), jnp.float32, least / len(cuts), high / len(cuts))
        return jnp.repeat(jnp.exp(draws), dims[dim] // parts).reshape((-1,) + (1,) * (len(dims) - dim - 1))

    gain = one(*cuts[0])
    for cut in cuts[1:]:
        gain = gain * one(*cut)
    return gain


def noise(rng, dims, scale, most, cuts=(), held_as=jnp.bfloat16):
    entries = jax.random.normal(rng, dims, jnp.float32) * scale
    if len(cuts) > 0:
        entries = shard_levels(rng, dims, cuts, -0.22, 0.18) * entries
    return jnp.clip(entries, min=-most, max=most).astype(held_as)


def setup_inputs(seed: int = 0, part: int = 0) -> dict:
    seeds = jax.random.split(jax.random.key(seed), 12)
    part_splits = jax.random.split(jax.random.fold_in(seeds[11], part), 12)
    latent = draw_latent(jax.random.fold_in(jax.random.fold_in(seeds[11], part), 71), part)
    in_weight = draw_in_weight(jax.random.fold_in(seeds[11], 71), part)
    in_bias = noise(seeds[2], (C,), 0.3, 1.5, ((0, 2),), jnp.float32)
    first_gain = jnp.clip(1.0 + 0.15 * jax.random.normal(seeds[3], (C,), jnp.float32), 0.25, 1.75)
    first_weight = noise(seeds[4], (9, 3 * C, C), (27 * C) ** -0.5, 0.0625, ((2, 2),))
    first_bias = noise(seeds[5], (C,), 0.3, 1.5, ((0, 2),), jnp.float32)
    second_gain = jnp.clip(1.0 + 0.15 * jax.random.normal(seeds[6], (C,), jnp.float32), 0.25, 1.75)
    second_weight = noise(seeds[7], (9, 3 * C, C), (27 * C) ** -0.5, 0.0625, ((2, 2),))
    second_bias = noise(seeds[8], (C,), 0.3, 1.5, ((0, 2),), jnp.float32)
    up_weight = noise(seeds[9], (3, 3 * C, CU), (9 * C) ** -0.5, 0.109375, ((2, 2),))
    up_bias = noise(seeds[10], (CU,), 0.3, 1.5, ((0, 2),), jnp.float32)
    return {"latent": latent, "in_weight": in_weight, "in_bias": in_bias, "first_gain": first_gain, "first_weight": first_weight, "first_bias": first_bias, "second_gain": second_gain, "second_weight": second_weight, "second_bias": second_bias, "up_weight": up_weight, "up_bias": up_bias}


epsilon = 1e-06

def width_taps(tap_slab):
    col_count = tap_slab.shape[-2] - 2
    return jnp.concatenate([tap_slab[..., 0:col_count, :], tap_slab[..., 1:col_count + 1, :], tap_slab[..., 2:col_count + 2, :]], axis=-1)

def conv_frames(padded, weight, tap_depth, frame_count):
    row_count = padded.shape[1] - 2
    col_count = padded.shape[2] - 2
    out_chan = weight.shape[-1]

    def one_frame(frame_at):
        window = lax.dynamic_slice_in_dim(padded, frame_at, tap_depth, 0)
        running = jnp.zeros((row_count * col_count, out_chan), jnp.float32)
        for tap_index in range(tap_depth * 3):
            row_at = tap_index % 3
            tap_slab = window[tap_index // 3, row_at:row_at + row_count]
            tap_cols = width_taps(tap_slab).reshape(row_count * col_count, -1)
            running = running + jnp.dot(tap_cols, weight[tap_index], preferred_element_type=jnp.float32)
        return running.reshape(row_count, col_count, out_chan)
    return lax.map(one_frame, jnp.arange(frame_count).astype(jnp.int32))

def activate(values, gain_vec):
    values = values.astype(jnp.float32)
    factor = lax.rsqrt(lax.optimization_barrier(jnp.mean(values * values, axis=-1, keepdims=True)) + epsilon)
    return jax.nn.silu(values * factor * gain_vec).astype(jnp.bfloat16)

def causal_pad(values):
    return jnp.pad(values, ((2, 0), (1, 1), (1, 1), (0, 0)))

def reference(latent, in_weight, in_bias, first_gain, first_weight, first_bias, second_gain, second_weight, second_bias, up_weight, up_bias):
    frame_count = SECTIONS * FS
    padded = causal_pad(latent.reshape(frame_count, LH, LW, ZC))

    def first_frame(frame_at):
        window = lax.dynamic_slice_in_dim(padded, frame_at, 3, 0)
        pieces = []
        for depth_at in range(3):
            for row_at in range(3):
                for col_at in range(3):
                    pieces.append(window[depth_at, row_at:row_at + LH, col_at:col_at + LW])
        tap_cols = jnp.concatenate(pieces, axis=-1).reshape(LH * LW, 27 * ZC)
        return jnp.dot(tap_cols, in_weight, preferred_element_type=jnp.float32).reshape(LH, LW, C)
    first_out = (lax.map(first_frame, jnp.arange(frame_count).astype(jnp.int32)) + in_bias).astype(jnp.bfloat16)
    first_act = activate(first_out, first_gain)
    second_out = (conv_frames(causal_pad(first_act), first_weight, 3, frame_count) + first_bias).astype(jnp.bfloat16)
    second_act = activate(second_out, second_gain)
    block_out = (first_out.astype(jnp.float32) + conv_frames(causal_pad(second_act), second_weight, 3, frame_count) + second_bias).astype(jnp.bfloat16)
    upsampled = jnp.repeat(jnp.repeat(block_out, 2, axis=1), 2, axis=2)
    upsampled = jnp.pad(upsampled, ((0, 0), (1, 1), (1, 1), (0, 0)))
    output = (conv_frames(upsampled, up_weight, 1, frame_count) + up_bias).astype(jnp.bfloat16)
    return jnp.transpose(output, (0, 1, 3, 2))
```

```python
import functools

import jax
import jax.numpy as jnp
from jax import lax
from jax.experimental import pallas as pl
from jax.experimental.pallas import tpu as pltpu
from jax.sharding import PartitionSpec as P

ZC = 16
C = 384
FS = 2
LW = 64
LANES = 128
WIDE = 256

epsilon = 1e-06


def activated(values, gain_half):
    squares = jnp.sum(values * values, axis=-1, keepdims=True)
    half = values * lax.rsqrt(squares * (1.0 / C) + epsilon) * gain_half
    return half + half * jnp.tanh(half)


def store_width_taps(target, frame, act, rows):
    act = act.reshape(rows, LW, C)
    column = lax.broadcasted_iota(jnp.int32, act.shape, 1)
    left = jnp.where(column == 0, 0.0, pltpu.roll(act, 1, 1))
    right = jnp.where(column == LW - 1, 0.0, pltpu.roll(act, LW - 1, 1))
    target[frame, :, :, 0:C] = left.astype(jnp.bfloat16)
    target[frame, :, :, C : 2 * C] = act.astype(jnp.bfloat16)
    target[frame, :, :, 2 * C :] = right.astype(jnp.bfloat16)


def masked_rows(act, rows, first_row, frame_ok, height):
    act = act.reshape(rows, LW, C)
    row = lax.broadcasted_iota(jnp.int32, act.shape, 0) + first_row
    keep = (row >= 0) & (row < height) & frame_ok
    return jnp.where(keep, act, 0.0).reshape(rows * LW, C)


def joined(low, high):
    lane = lax.broadcasted_iota(jnp.int32, (low.shape[0], LANES), 1)
    middle = jnp.where(lane < LANES // 2, low[:, LANES:], high[:, :LANES])
    return jnp.concatenate([low[:, :LANES], middle, high[:, LANES:]], axis=-1)


def packed(half, chan):
    return jnp.where(chan == 0, half, pltpu.roll(half, WIDE - C // 2, 1))


def halves(own, other, chan):
    own = own.astype(jnp.float32)
    other = other.astype(jnp.float32)
    return joined(jnp.where(chan == 0, own, other), jnp.where(chan == 0, other, own))


def conv_into(acc, taps, weight, starts, out_frames, out_rows):
    width = weight.shape[1]
    block = out_rows * LW
    acc[:, 0:width] = jnp.zeros((acc.shape[0], width), jnp.float32)
    for depth_at in (2, 1, 0):
        skip = max(0, -(starts + depth_at))
        count = out_frames - skip
        if count <= 0:
            continue
        first = starts + depth_at + skip
        for row_at in range(3):
            lhs = taps[first : first + count, row_at : row_at + out_rows]
            product = lax.dot_general(
                lhs.reshape(count * block, 3 * C),
                weight[depth_at * 3 + row_at],
                (((1,), (1,)), ((), ())),
                preferred_element_type=jnp.float32,
            )
            acc[skip * block :, 0:width] += product


def first_stage(
    dims, lat, win, bias, gain, weight, conv_bias, second, residual, window, taps, acc
):
    tm_count, rows_here, height, early = dims
    early_in, early_one, early_two = early
    space = lax.axis_index("space")
    section = lax.axis_index("tm")
    chan = lax.axis_index("chan")
    row0 = space * rows_here
    groups = LW * ZC // LANES
    lane = lax.broadcasted_iota(jnp.int32, (groups, LANES), 1)
    group = lax.broadcasted_iota(jnp.int32, (groups, LANES), 0)
    low = lane < LANES // 2
    frames_in = FS + early_in
    rows_in = rows_here + 8

    for frame in range(frames_in):
        frame_abs = section * FS - early_in + frame
        for row in range(rows_in):
            row_abs = row0 - 4 + row
            ok = (frame_abs >= 0) & (row_abs >= 0) & (row_abs < height)
            at = jnp.where(ok, frame_abs * height + row_abs, 0)
            here = jnp.where(ok, lat[at], 0.0)
            before = jnp.where(group == 0, 0.0, pltpu.roll(here, 1, 0))
            after = jnp.where(group == groups - 1, 0.0, pltpu.roll(here, groups - 1, 0))
            for col in range(8):
                source = here
                if col == 0:
                    source = jnp.where(lane >= LANES - ZC, before, here)
                if col == 7:
                    source = jnp.where(lane < ZC, after, here)
                shift = (-ZC * (col - 1)) % LANES
                one = source if shift == 0 else pltpu.roll(source, shift, 1)
                two = pltpu.roll(source, (shift + LANES // 2) % LANES, 1)
                window.at[frame, row][pl.ds(col, groups, stride=8), :] = jnp.where(low, one, two)

    rows_one = rows_here + 6
    voxels = rows_one * LW
    lane_wide = lax.broadcasted_iota(jnp.int32, (rows_one, LW, LANES), 2)
    half_gain = gain[...] * 0.5
    for frame in range(FS + early_one):
        slots = []
        for depth_at in (2, 1, 0):
            source = frame - early_one - 2 + depth_at + early_in
            if source >= 0:
                slots += [(source, row_at) for row_at in range(3)]
        pieces = []
        for pair in range(0, len(slots), 2):
            source, row_at = slots[pair]
            value = window[source, row_at : row_at + rows_one]
            second_slot = 0.0
            if pair + 1 < len(slots):
                source, row_at = slots[pair + 1]
                second_slot = window[source, row_at : row_at + rows_one]
            value = jnp.where(lane_wide < LANES // 2, value, second_slot)
            pieces.append(value.astype(jnp.bfloat16).reshape(voxels, LANES))
        lhs = jnp.concatenate(pieces, axis=-1)
        out = jnp.dot(lhs, win[0 : lhs.shape[1]], preferred_element_type=jnp.float32)
        out = (out + bias[...]).astype(jnp.bfloat16)
        if frame >= early_one:
            inner = out[2 * LW : (rows_one - 2) * LW].astype(jnp.float32)
            mine = jnp.where(
                chan == 0, inner[:, :WIDE], pltpu.roll(inner[:, LANES:], C // 2, 1)
            )
            residual[frame - early_one] = mine.astype(jnp.bfloat16)
        act = activated(out.astype(jnp.float32), half_gain)
        frame_ok = section * FS - early_one + frame >= 0
        act = masked_rows(act, rows_one, row0 - 3, frame_ok, height)
        store_width_taps(taps, frame, act, rows_one)

    conv_into(
        acc, taps, weight, early_one - early_two - 2, FS + early_two, rows_here + 4
    )
    second[...] = packed(acc[...] + conv_bias[...], chan).astype(jnp.bfloat16)


def second_stage(
    dims, own, other, residual, gain, weight, conv_bias, block, taps, acc
):
    tm_count, rows_here, height, early_two = dims
    section = lax.axis_index("tm")
    chan = lax.axis_index("chan")
    row0 = lax.axis_index("space") * rows_here
    rows_two = rows_here + 4
    voxels = rows_two * LW
    half_gain = gain[...] * 0.5
    for frame in range(FS + early_two):
        span = pl.ds(frame * voxels, voxels)
        values = halves(own[span, :], other[span, :], chan)
        act = activated(values, half_gain)
        frame_ok = section * FS - early_two + frame >= 0
        act = masked_rows(act, rows_two, row0 - 2, frame_ok, height)
        store_width_taps(taps, frame, act, rows_two)
    conv_into(acc, taps, weight, early_two - 2, FS, rows_here + 2)
    total = acc[...] + conv_bias[...] + residual[...].astype(jnp.float32)
    block[...] = packed(total, chan).astype(jnp.bfloat16)


def third_stage(dims, own, other, weight, up_bias, decoded, taps):
    rows_here, height = dims
    chan = lax.axis_index("chan")
    row0 = lax.axis_index("space") * rows_here
    rows_three = rows_here + 2
    voxels = rows_three * LW
    out_chan = weight.shape[2] // 2
    for frame in range(FS):
        span = pl.ds(frame * voxels, voxels)
        values = halves(own[span, :], other[span, :], chan)
        values = masked_rows(values, rows_three, row0 - 1, True, height)
        store_width_taps(taps, frame, values, rows_three)
    count = FS * rows_here * LW
    source = lax.broadcasted_iota(jnp.int32, (4 * LW, 4 * LW), 0)
    target = lax.broadcasted_iota(jnp.int32, (4 * LW, 4 * LW), 1)
    phase = source // (2 * LW)
    place = source % (2 * LW)
    wanted = (place // LW) * (2 * LW) + (place % LW) * 2 + phase
    shuffle = jnp.where(wanted == target, 1.0, 0.0).astype(jnp.bfloat16)
    for row_phase in range(2):
        total = jnp.zeros((2 * out_chan, count), jnp.float32)
        for row_at in range(2):
            at = row_phase + row_at
            lhs = taps[:, at : at + rows_here].reshape(count, 3 * C)
            total = total + lax.dot_general(
                weight[row_phase, row_at],
                lhs,
                (((1,), (1,)), ((), ())),
                preferred_element_type=jnp.float32,
            )
        for frame in range(FS):
            for row in range(0, rows_here, 2):
                start = (frame * rows_here + row) * LW
                part = total[:, start : start + 2 * LW]
                pair = jnp.concatenate([part[:out_chan], part[out_chan:]], axis=-1)
                pair = (pair + up_bias[...]).astype(jnp.bfloat16)
                pixels = jnp.dot(pair, shuffle, preferred_element_type=jnp.float32)
                pixels = pixels.astype(jnp.bfloat16)
                decoded[frame, 2 * row + row_phase] = pixels[:, : 2 * LW]
                decoded[frame, 2 * row + 2 + row_phase] = pixels[:, 2 * LW :]


def in_vmem(count):
    return [pl.BlockSpec(memory_space=pltpu.VMEM)] * count


def up_phases(up_weight):
    w = jnp.swapaxes(up_weight, 1, 2).astype(jnp.float32)
    w = [[w[b, :, c * C : (c + 1) * C] for c in range(3)] for b in range(3)]
    out = []
    for top, bottom in (((0,), (1, 2)), ((0, 1), (2,))):
        for rows in (top, bottom):
            cols = [sum(w[b][c] for b in rows) for c in range(3)]
            zero = jnp.zeros_like(cols[0])
            even = jnp.concatenate([cols[0], cols[1] + cols[2], zero], axis=1)
            odd = jnp.concatenate([zero, cols[0] + cols[1], cols[2]], axis=1)
            out.append(jnp.concatenate([even, odd], axis=0))
    return jnp.stack(out).reshape(2, 2, -1, 3 * C).astype(jnp.bfloat16)


def shards(
    latent,
    in_weight,
    in_bias,
    first_gain,
    first_weight,
    first_bias,
    second_gain,
    second_weight,
    second_bias,
    up_weight,
    up_bias,
):
    space_count = lax.axis_size("space")
    tm_count = lax.axis_size("tm")
    chan = lax.axis_index("chan")
    rows_here = latent.shape[1] // FS
    height = rows_here * space_count
    groups = LW * ZC // LANES
    half = C // 2
    earlier = FS * (tm_count - 1)
    early_two, early_one, early_in = min(2, earlier), min(4, earlier), min(6, earlier)
    swap = [(0, 1), (1, 0)]

    piece = latent.reshape(1, FS * rows_here * groups, LANES).astype(jnp.float32)
    piece = jnp.broadcast_to(piece, (tm_count * space_count,) + piece.shape[1:])
    lat = lax.all_to_all(piece, ("tm", "space"), 0, 0, tiled=True)
    lat = lat.reshape(tm_count * FS * height, groups, LANES)

    other_weight = lax.ppermute(in_weight, "chan", swap)
    other_bias = lax.ppermute(in_bias, "chan", swap)
    win = jnp.where(
        chan == 0,
        jnp.concatenate([in_weight, other_weight], axis=1),
        jnp.concatenate([other_weight, in_weight], axis=1),
    )
    win = win.reshape(3, 3, 3 * ZC, C)[::-1].reshape(9, 3 * ZC, C)
    win = jnp.pad(win, ((0, 1), (0, LANES // 2 - 3 * ZC), (0, 0))).reshape(5 * LANES, C)
    bias = jnp.where(
        chan == 0,
        jnp.concatenate([in_bias, other_bias]),
        jnp.concatenate([other_bias, in_bias]),
    ).reshape(1, C)

    def wide(vector):
        return jnp.pad(vector, (0, WIDE - half)).reshape(1, WIDE)

    voxels_two = (FS + early_two) * (rows_here + 4) * LW
    voxels_three = FS * (rows_here + 2) * LW
    second_own, residual = pl.pallas_call(
        functools.partial(
            first_stage, (tm_count, rows_here, height, (early_in, early_one, early_two))
        ),
        out_shape=(
            jax.ShapeDtypeStruct((voxels_two, WIDE), jnp.bfloat16),
            jax.ShapeDtypeStruct((FS, (rows_here + 2) * LW, WIDE), jnp.bfloat16),
        ),
        in_specs=in_vmem(6),
        out_specs=tuple(in_vmem(2)),
        scratch_shapes=[
            pltpu.VMEM((FS + early_in, rows_here + 8, LW, LANES), jnp.float32),
            pltpu.VMEM((FS + early_one, rows_here + 6, LW, 3 * C), jnp.bfloat16),
            pltpu.VMEM((voxels_two, WIDE), jnp.float32),
        ],
        name="first_stage",
    )(lat, win, bias, first_gain.reshape(1, C), jnp.swapaxes(first_weight, 1, 2), wide(first_bias))
    second_other = lax.ppermute(second_own, "chan", swap)

    block_own = pl.pallas_call(
        functools.partial(second_stage, (tm_count, rows_here, height, early_two)),
        out_shape=jax.ShapeDtypeStruct((voxels_three, WIDE), jnp.bfloat16),
        in_specs=in_vmem(6),
        out_specs=in_vmem(1)[0],
        scratch_shapes=[
            pltpu.VMEM((FS + early_two, rows_here + 4, LW, 3 * C), jnp.bfloat16),
            pltpu.VMEM((voxels_three, WIDE), jnp.float32),
        ],
        name="second_stage",
    )(
        second_own,
        second_other,
        residual.reshape(voxels_three, WIDE),
        second_gain.reshape(1, C),
        jnp.swapaxes(second_weight, 1, 2),
        wide(second_bias),
    )
    block_other = lax.ppermute(block_own, "chan", swap)

    out_chan = up_weight.shape[-1]
    return pl.pallas_call(
        functools.partial(third_stage, (rows_here, height)),
        out_shape=jax.ShapeDtypeStruct((FS, 2 * rows_here, out_chan, 2 * LW), jnp.bfloat16),
        in_specs=in_vmem(4),
        out_specs=in_vmem(1)[0],
        scratch_shapes=[pltpu.VMEM((FS, rows_here + 2, LW, 3 * C), jnp.bfloat16)],
        name="third_stage",
    )(block_own, block_other, up_phases(up_weight), up_bias.reshape(out_chan, 1))


def solution(mesh):
    placed = (
        P(("groups", "tm"), "space", None),
        P(None, "chan"),
        P("chan"),
        P(),
        P(None, None, "chan"),
        P("chan"),
        P(),
        P(None, None, "chan"),
        P("chan"),
        P(None, None, "chan"),
        P("chan"),
    )
    return jax.shard_map(
        shards,
        mesh=mesh,
        in_specs=placed,
        out_specs=P(("groups", "tm"), "space", "chan", None),
        check_vma=False,
    )
```

```python
import functools

import jax
import jax.numpy as jnp
from jax import lax
from jax.experimental import pallas as pl
from jax.experimental.pallas import tpu as pltpu
from jax.sharding import PartitionSpec as P

ZC = 16
C = 384
FS = 2
LW = 64
LANES = 128
WIDE = 256

epsilon = 1e-06


def row_of(vector):
    return vector[...].reshape(1, vector.shape[0])


def wide_of(vector):
    row = row_of(vector)
    return jnp.concatenate([row, jnp.zeros((1, WIDE - C // 2), row.dtype)], axis=-1)


def activated(values, gain_half, keep):
    squares = jnp.sum(values * values, axis=-1, keepdims=True)
    factor = lax.rsqrt(squares * (1.0 / C) + epsilon) * keep
    half = values * factor * gain_half
    return half + half * jnp.tanh(half)


def kept(frame_ok, row, height):
    return jnp.where(frame_ok & (row >= 0) & (row < height), 1.0, 0.0)


def joined(low, high):
    lane = lax.broadcasted_iota(jnp.int32, (low.shape[0], LANES), 1)
    middle = jnp.where(lane < LANES // 2, low[:, LANES:], high[:, :LANES])
    return jnp.concatenate([low[:, :LANES], middle, high[:, LANES:]], axis=-1)


def packed(half, chan):
    return jnp.where(chan == 0, half, pltpu.roll(half, WIDE - C // 2, 1))


def halves(own, other, chan):
    low = jnp.where(chan == 0, own, other)
    high = jnp.where(chan == 0, other, own)
    return joined(low.astype(jnp.float32), high.astype(jnp.float32))


def conv_part(acts, weight, places, frames, rows, col):
    lhs, rhs = [], []
    for depth_at, row_at, frame in places:
        piece = acts[frame : frame + frames, row_at : row_at + rows]
        lhs.append(piece.reshape(frames * rows * LW, C))
        rhs.append(weight[depth_at * 3 + row_at, :, col * C : (col + 1) * C])
    return lax.dot_general(
        jnp.concatenate(lhs, axis=1),
        jnp.concatenate(rhs, axis=1),
        (((1,), (1,)), ((), ())),
        preferred_element_type=jnp.float32,
    )


def columns_summed(parts, span):
    left, here, right = (parts[col, span, :] for col in range(3))
    column = lax.broadcasted_iota(jnp.int32, left.shape, 0)
    left = jnp.where(column == 0, 0.0, pltpu.roll(left, 1, 0))
    right = jnp.where(column == LW - 1, 0.0, pltpu.roll(right, LW - 1, 0))
    return left + here + right


def first_stage(dims, *refs):
    rows_here, height, early, plan = dims
    early_in, early_one, early_two = early
    chunks, refs = list(refs[: len(plan)]), refs[len(plan) :]
    win, bias, gain_in, weight_in, conv_bias_in, second, residual, *refs = refs
    rows, window, pre, acts, parts, own, gain, conv_bias, weight, sems = refs
    fetches = []
    for source, target in (
        (chunks[0], own),
        (gain_in, gain),
        (conv_bias_in, conv_bias),
        (weight_in, weight),
    ):
        fetch = pltpu.make_async_copy(source, target, sems.at[len(fetches)])
        fetch.start()
        fetches.append(fetch)
    space = lax.axis_index("space")
    section = lax.axis_index("tm")
    chan = lax.axis_index("chan")
    row0 = space * rows_here
    groups = LW * ZC // LANES
    lane = lax.broadcasted_iota(jnp.int32, (groups, LANES), 1)
    group = lax.broadcasted_iota(jnp.int32, (groups, LANES), 0)
    low = lane < LANES // 2
    rows_in = rows_here + 8

    fetches[0].wait()
    chunks[0] = own
    for chunk, (back, turn) in zip(chunks, plan):
        count = chunk.shape[0]
        start = early_in // FS * FS * height - back * FS * height
        if turn is not None:
            blocks = FS * height // count
            start = start + lax.rem(space + (blocks - turn), blocks) * count
        values = chunk[...].astype(jnp.float32)
        for at in range(groups):
            rows[pl.ds(start, count), at, :] = values[:, at * LANES : (at + 1) * LANES]

    for frame in range(FS + early_in):
        frame_ok = section * FS - early_in + frame >= 0
        for row in range(rows_in):
            row_abs = row0 - 4 + row
            ok = frame_ok & (row_abs >= 0) & (row_abs < height)
            at = frame * height + jnp.clip(row_abs, 0, height - 1)
            here = jnp.where(ok, rows[at], 0.0)
            before = jnp.where(group == 0, 0.0, pltpu.roll(here, 1, 0))
            after = jnp.where(group == groups - 1, 0.0, pltpu.roll(here, groups - 1, 0))
            for col in range(8):
                source = here
                if col == 0:
                    source = jnp.where(lane >= LANES - ZC, before, here)
                if col == 7:
                    source = jnp.where(lane < ZC, after, here)
                shift = (-ZC * (col - 1)) % LANES
                one = source if shift == 0 else pltpu.roll(source, shift, 1)
                two = pltpu.roll(source, (shift + LANES // 2) % LANES, 1)
                window.at[frame, row][pl.ds(col, groups, stride=8), :] = jnp.where(low, one, two)

    rows_one = rows_here + 6
    rows_two = rows_here + 4
    lane_wide = lax.broadcasted_iota(jnp.int32, (rows_one, LW, LANES), 2)

    def input_conv(frame):
        slots = []
        for depth_at in (2, 1, 0):
            source = frame - early_one - 2 + depth_at + early_in
            if source >= 0:
                slots += [(source, row_at) for row_at in range(3)]
        pieces = []
        for pair in range(0, len(slots), 2):
            source, row_at = slots[pair]
            value = window[source, row_at : row_at + rows_one]
            second_slot = 0.0
            if pair + 1 < len(slots):
                source, row_at = slots[pair + 1]
                second_slot = window[source, row_at : row_at + rows_one]
            value = jnp.where(lane_wide < LANES // 2, value, second_slot)
            pieces.append(value.astype(jnp.bfloat16).reshape(rows_one * LW, LANES))
        lhs = jnp.concatenate(pieces, axis=-1)
        pre[frame % 2] = jnp.dot(
            lhs, win[0 : lhs.shape[1]], preferred_element_type=jnp.float32
        )

    def activate(frame, row):
        frame_ok = section * FS - early_one + frame >= 0
        out = pre[frame % 2, row * LW : (row + 1) * LW] + bias[...]
        out = out.astype(jnp.bfloat16).astype(jnp.float32)
        if frame >= early_one and 2 <= row < rows_one - 2:
            mine = jnp.where(chan == 0, out[:, :WIDE], pltpu.roll(out[:, LANES:], C // 2, 1))
            span = pl.ds((row - 2) * LW, LW)
            residual[frame - early_one, span, :] = mine.astype(jnp.bfloat16)
        keep = kept(frame_ok, row0 - 3 + row, height)
        act = activated(out, row_of(gain) * 0.5, keep)
        acts[frame, row] = act.astype(jnp.bfloat16)

    def convolve(frame, col):
        places = []
        for depth_at in (2, 1, 0):
            source = frame - early_two - 2 + depth_at + early_one
            if source >= 0:
                places += [(depth_at, row_at, source) for row_at in range(3)]
        product = conv_part(acts, weight, places, 1, rows_two, col)
        parts[frame % 2, col, :, 0 : C // 2] = product

    def finish(frame):
        for row in range(rows_two):
            total = columns_summed(parts.at[frame % 2], pl.ds(row * LW, LW))
            total = packed(total + wide_of(conv_bias), chan)
            span = pl.ds((frame * rows_two + row) * LW, LW)
            second[span, :] = total.astype(jnp.bfloat16)

    lead = early_one - early_two
    frames_one = FS + early_one
    fetches[1].wait()
    fetches[2].wait()
    for frame in range(lead + 1):
        input_conv(frame)
        for row in range(rows_one):
            activate(frame, row)
    fetches[3].wait()
    for frame in range(FS + early_two):
        later = frame + lead + 1
        row = 0
        if later < frames_one:
            input_conv(later)
        for col in range(3):
            convolve(frame, col)
            while later < frames_one and row * 3 < rows_one * (col + 1):
                activate(later, row)
                row += 1
        finish(frame)


def second_stage(dims, own, other, residual, gain, weight, conv_bias, block, acts, parts):
    rows_here, height, early_two = dims
    section = lax.axis_index("tm")
    chan = lax.axis_index("chan")
    row0 = lax.axis_index("space") * rows_here
    rows_two = rows_here + 4
    rows_three = rows_here + 2
    frames_two = FS + early_two

    def activate(frame):
        frame_ok = section * FS - early_two + frame >= 0
        half_gain = row_of(gain) * 0.5
        for row in range(rows_two):
            span = pl.ds((frame * rows_two + row) * LW, LW)
            values = halves(own[span, :], other[span, :], chan)
            act = activated(values, half_gain, kept(frame_ok, row0 - 2 + row, height))
            acts[frame, row] = act.astype(jnp.bfloat16)

    done = 0
    first = True
    for depth_at in range(3):
        skip = max(0, 2 - early_two - depth_at)
        count = FS - skip
        if count <= 0:
            continue
        start = skip - 2 + depth_at + early_two
        while done < start + count:
            activate(done)
            done += 1
        places = [(depth_at, row_at, start) for row_at in range(3)]
        from_row = skip * rows_three * LW
        for col in range(3):
            product = conv_part(acts, weight, places, count, rows_three, col)
            if first:
                if from_row:
                    parts[col, 0:from_row, :] = jnp.zeros((from_row, WIDE), jnp.float32)
                parts[col, from_row:, 0 : C // 2] = product
            else:
                parts[col, from_row:, 0 : C // 2] += product
        first = False
    for row in range(FS * rows_three):
        span = pl.ds(row * LW, LW)
        total = columns_summed(parts, span) + wide_of(conv_bias)
        total = total + residual[span, :].astype(jnp.float32)
        block[span, :] = packed(total, chan).astype(jnp.bfloat16)


def third_stage(dims, own, other, weight, up_bias, decoded, acts, raw):
    rows_here, height = dims
    chan = lax.axis_index("chan")
    row0 = lax.axis_index("space") * rows_here
    rows_three = rows_here + 2
    out_chan = weight.shape[1] // 4
    for frame in range(FS):
        for row in range(rows_three):
            span = pl.ds((frame * rows_three + row) * LW, LW)
            values = halves(own[span, :], other[span, :], chan)
            values = values * kept(True, row0 - 1 + row, height)
            acts[frame, row] = values.astype(jnp.bfloat16)
    count = FS * rows_here * LW
    source = lax.broadcasted_iota(jnp.int32, (4 * LW, 4 * LW), 0)
    target = lax.broadcasted_iota(jnp.int32, (4 * LW, 4 * LW), 1)
    phase = source // (2 * LW)
    place = source % (2 * LW)
    wanted = (place // LW) * (2 * LW) + (place % LW) * 2 + phase
    shuffle = jnp.where(wanted == target, 1.0, 0.0).astype(jnp.bfloat16)
    column_bias = row_of(up_bias).T
    column = lax.broadcasted_iota(jnp.int32, (out_chan, 2 * LW), 1) % LW
    for row_phase in range(2):
        lhs = [
            acts[:, at : at + rows_here].reshape(count, C)
            for at in (row_phase, row_phase + 1)
        ]
        raw[row_phase] = lax.dot_general(
            weight[row_phase],
            jnp.concatenate(lhs, axis=1),
            (((1,), (1,)), ((), ())),
            preferred_element_type=jnp.float32,
        )
        pairs = []
        for start in range(0, count, 2 * LW):
            left, even, odd, right = (
                raw[row_phase, at * out_chan : (at + 1) * out_chan, start : start + 2 * LW]
                for at in range(4)
            )
            left = jnp.where(column == 0, 0.0, pltpu.roll(left, 1, 1))
            right = jnp.where(column == LW - 1, 0.0, pltpu.roll(right, 2 * LW - 1, 1))
            pair = jnp.concatenate([left + even + column_bias, odd + right + column_bias], axis=1)
            pairs.append(pair.astype(jnp.bfloat16))
        pixels = jnp.dot(
            jnp.concatenate(pairs, axis=0), shuffle, preferred_element_type=jnp.float32
        ).astype(jnp.bfloat16)
        for at in range(len(pairs)):
            frame, row = divmod(2 * at, rows_here)
            part = pixels[at * out_chan : (at + 1) * out_chan]
            decoded[frame, 2 * row + row_phase] = part[:, : 2 * LW]
            decoded[frame, 2 * row + 2 + row_phase] = part[:, 2 * LW :]


def prepare(own_in, other_in, own_bias, other_bias, up_in, win, bias, phases, own, own_b, up, sems):
    fetches = []
    for source, target in ((own_in, own), (own_bias, own_b), (up_in, up)):
        fetch = pltpu.make_async_copy(source, target, sems.at[len(fetches)])
        fetch.start()
        fetches.append(fetch)
    chan = lax.axis_index("chan")
    fetches[0].wait()
    fetches[1].wait()
    mine, other = own[...].astype(jnp.float32), other_in[...].astype(jnp.float32)
    low = jnp.where(chan == 0, mine, other)
    high = jnp.where(chan == 0, other, mine)
    joint = jnp.concatenate([low, high], axis=0).T.astype(jnp.bfloat16)
    blank = jnp.zeros((LANES // 2, C), jnp.bfloat16)
    for slot in range(10):
        win[slot * 64 : slot * 64 + 64, :] = blank
    for slot in range(9):
        source = ((2 - slot // 3) * 3 + slot % 3) * 3 * ZC
        win[slot * 64 : slot * 64 + 3 * ZC, :] = joint[source : source + 3 * ZC]
    mine_b, other_b = row_of(own_b), row_of(other_bias)
    low = jnp.where(chan == 0, mine_b, other_b)
    high = jnp.where(chan == 0, other_b, mine_b)
    bias[...] = jnp.concatenate([low, high], axis=1)
    fetches[2].wait()
    count = up.shape[1]
    for row_phase, split in enumerate((((0,), (1, 2)), ((0, 1), (2,)))):
        for row_at, taps in enumerate(split):
            cols = []
            for c in range(3):
                cut = pl.ds(c * C, C)
                value = up[taps[0], :, cut].astype(jnp.float32)
                for tap in taps[1:]:
                    value = value + up[tap, :, cut].astype(jnp.float32)
                cols.append(value)
            grouped = (cols[0], cols[1] + cols[2], cols[0] + cols[1], cols[2])
            for at, value in enumerate(grouped):
                target = (row_phase, pl.ds(at * count, count), pl.ds(row_at * C, C))
                phases[target] = value.astype(jnp.bfloat16)


def limits(mib):
    return pltpu.CompilerParams(vmem_limit_bytes=mib * 1024 * 1024)


def shards(
    latent,
    in_weight,
    in_bias,
    first_gain,
    first_weight,
    first_bias,
    second_gain,
    second_weight,
    second_bias,
    up_weight,
    up_bias,
):
    space_count = lax.axis_size("space")
    tm_count = lax.axis_size("tm")
    rows_here = latent.shape[1] // FS
    height = rows_here * space_count
    groups = LW * ZC // LANES
    earlier = FS * (tm_count - 1)
    early_two, early_one, early_in = min(2, earlier), min(4, earlier), min(6, earlier)
    swap = [(0, 1), (1, 0)]

    plan = []
    if space_count <= 4:
        section_chunks = [latent[0]]
        for turn in range(1, space_count):
            pairs = [(i, (i + turn) % space_count) for i in range(space_count)]
            section_chunks.append(lax.ppermute(latent[0], "space", pairs))
        turns = list(range(space_count))
    else:
        section_chunks = [lax.all_gather(latent[0], "space", axis=0, tiled=True)]
        turns = [None]
    chunks = list(section_chunks)
    plan = [(0, turn) for turn in turns]
    for back in range(1, early_in // FS + 1):
        pairs = [(i, (i + back) % tm_count) for i in range(tm_count)]
        for chunk, turn in zip(section_chunks, turns):
            chunks.append(lax.ppermute(chunk, "tm", pairs))
            plan.append((back, turn))

    stored_in = jnp.swapaxes(in_weight, 0, 1)
    stored_up = jnp.swapaxes(up_weight, 1, 2)
    out_chan = up_weight.shape[-1]
    def stay(array):
        return pltpu.with_memory_space_constraint(array, pltpu.HBM)

    vmem, hbm = pl.BlockSpec(memory_space=pltpu.VMEM), pl.BlockSpec(memory_space=pltpu.HBM)
    win, bias, phases = pl.pallas_call(
        prepare,
        out_shape=(
            jax.ShapeDtypeStruct((5 * LANES, C), jnp.bfloat16),
            jax.ShapeDtypeStruct((1, C), jnp.float32),
            jax.ShapeDtypeStruct((2, 4 * out_chan, 2 * C), jnp.bfloat16),
        ),
        in_specs=[hbm, vmem, hbm, vmem, hbm],
        out_specs=(vmem,) * 3,
        scratch_shapes=[
            pltpu.VMEM(stored_in.shape, jnp.bfloat16),
            pltpu.VMEM(in_bias.shape, jnp.float32),
            pltpu.VMEM(stored_up.shape, jnp.bfloat16),
            pltpu.SemaphoreType.DMA((3,)),
        ],
        compiler_params=limits(12),
        name="prepare",
    )(
        stay(stored_in),
        lax.ppermute(stored_in, "chan", swap),
        stay(in_bias),
        lax.ppermute(in_bias, "chan", swap),
        stay(stored_up),
    )

    voxels_two = (FS + early_two) * (rows_here + 4) * LW
    voxels_three = FS * (rows_here + 2) * LW
    early = (early_in, early_one, early_two)
    stored_first = jnp.swapaxes(first_weight, 1, 2)
    second_own, residual = pl.pallas_call(
        functools.partial(first_stage, (rows_here, height, early, tuple(plan))),
        out_shape=(
            jax.ShapeDtypeStruct((voxels_two, WIDE), jnp.bfloat16),
            jax.ShapeDtypeStruct((FS, (rows_here + 2) * LW, WIDE), jnp.bfloat16),
        ),
        in_specs=[hbm] + [vmem] * (len(chunks) + 1) + [hbm] * 3,
        out_specs=(vmem,) * 2,
        scratch_shapes=[
            pltpu.VMEM(((FS + early_in) * height, groups, LANES), jnp.float32),
            pltpu.VMEM((FS + early_in, rows_here + 8, LW, LANES), jnp.float32),
            pltpu.VMEM((2, (rows_here + 6) * LW, C), jnp.float32),
            pltpu.VMEM((FS + early_one, rows_here + 6, LW, C), jnp.bfloat16),
            pltpu.VMEM((2, 3, (rows_here + 4) * LW, WIDE), jnp.float32),
            pltpu.VMEM(chunks[0].shape, jnp.bfloat16),
            pltpu.VMEM(first_gain.shape, jnp.float32),
            pltpu.VMEM(first_bias.shape, jnp.float32),
            pltpu.VMEM(stored_first.shape, jnp.bfloat16),
            pltpu.SemaphoreType.DMA((4,)),
        ],
        compiler_params=limits(28),
        name="first_stage",
    )(
        stay(chunks[0]),
        *chunks[1:],
        win,
        bias,
        stay(first_gain),
        stay(stored_first),
        stay(first_bias),
    )
    second_other = lax.ppermute(second_own, "chan", swap)

    block_own = pl.pallas_call(
        functools.partial(second_stage, (rows_here, height, early_two)),
        out_shape=jax.ShapeDtypeStruct((voxels_three, WIDE), jnp.bfloat16),
        in_specs=[vmem] * 6,
        out_specs=vmem,
        scratch_shapes=[
            pltpu.VMEM((FS + early_two, rows_here + 4, LW, C), jnp.bfloat16),
            pltpu.VMEM((3, voxels_three, WIDE), jnp.float32),
        ],
        compiler_params=limits(16),
        name="second_stage",
    )(
        second_own,
        second_other,
        residual.reshape(voxels_three, WIDE),
        second_gain,
        jnp.swapaxes(second_weight, 1, 2),
        second_bias,
    )
    block_other = lax.ppermute(block_own, "chan", swap)

    return pl.pallas_call(
        functools.partial(third_stage, (rows_here, height)),
        out_shape=jax.ShapeDtypeStruct((FS, 2 * rows_here, out_chan, 2 * LW), jnp.bfloat16),
        in_specs=[vmem] * 4,
        out_specs=vmem,
        scratch_shapes=[
            pltpu.VMEM((FS, rows_here + 2, LW, C), jnp.bfloat16),
            pltpu.VMEM((2, 4 * out_chan, FS * rows_here * LW), jnp.float32),
        ],
        compiler_params=limits(12),
        name="third_stage",
    )(block_own, block_other, phases, up_bias)


def solution(mesh):
    placed = (
        P(("groups", "tm"), "space", None),
        P(None, "chan"),
        P("chan"),
        P(),
        P(None, None, "chan"),
        P("chan"),
        P(),
        P(None, None, "chan"),
        P("chan"),
        P(None, None, "chan"),
        P("chan"),
    )
    return jax.shard_map(
        shards,
        mesh=mesh,
        in_specs=placed,
        out_specs=P(("groups", "tm"), "space", "chan", None),
        check_vma=False,
    )
```

```python
import functools

import jax
import jax.numpy as jnp
from jax import lax
from jax.experimental import pallas as pl
from jax.experimental.pallas import tpu as pltpu
from jax.sharding import PartitionSpec as P

ZC = 16
C = 384
FS = 2
LW = 64
LANES = 128
WIDE = 256

epsilon = 1e-06


def row_of(vector):
    return vector[...].reshape(1, vector.shape[0])


def wide_of(vector):
    row = row_of(vector)
    return jnp.concatenate([row, jnp.zeros((1, WIDE - C // 2), row.dtype)], axis=-1)


def activated(values, gain_half, keep):
    squares = jnp.sum(values * values, axis=-1, keepdims=True)
    factor = lax.rsqrt(squares * (1.0 / C) + epsilon) * keep
    half = values * factor * gain_half
    return half + half * jnp.tanh(half)


def kept(frame_ok, row, height):
    return jnp.where(frame_ok & (row >= 0) & (row < height), 1.0, 0.0)


def joined(low, high):
    lane = lax.broadcasted_iota(jnp.int32, (low.shape[0], LANES), 1)
    middle = jnp.where(lane < LANES // 2, low[:, LANES:], high[:, :LANES])
    return jnp.concatenate([low[:, :LANES], middle, high[:, LANES:]], axis=-1)


def packed(half, chan):
    return jnp.where(chan == 0, half, pltpu.roll(half, WIDE - C // 2, 1))


def halves(own, other, chan):
    low = jnp.where(chan == 0, own, other)
    high = jnp.where(chan == 0, other, own)
    return joined(low.astype(jnp.float32), high.astype(jnp.float32))


def conv_part(piece, weight, places, col):
    lhs = [piece(place) for place in places]
    cut = slice(col * C, (col + 1) * C)
    rhs = [weight[depth_at * 3 + row_at, :, cut] for depth_at, row_at in places]
    return lax.dot_general(
        jnp.concatenate(lhs, axis=1),
        jnp.concatenate(rhs, axis=1),
        (((1,), (1,)), ((), ())),
        preferred_element_type=jnp.float32,
    )


def columns_summed(parts, span):
    left, here, right = (parts[col, span, :] for col in range(3))
    column = lax.broadcasted_iota(jnp.int32, left.shape, 0)
    left = jnp.where(column == 0, 0.0, pltpu.roll(left, 1, 0))
    right = jnp.where(column == LW - 1, 0.0, pltpu.roll(right, LW - 1, 0))
    return left + here + right


def first_stage(dims, *refs):
    rows_here, height, early, plan = dims
    early_in, early_one, early_two = early
    chunks, refs = list(refs[: len(plan)]), refs[len(plan) :]
    win, other_bias, weight, own_bias_in, gain_in, conv_bias_in, *refs = refs
    second, residual, acts, rows, window, pre, parts, *refs = refs
    own, own_bias, gain, conv_bias, sems = refs
    fetches = []
    for source, target in (
        (chunks[0], own),
        (own_bias_in, own_bias),
        (gain_in, gain),
        (conv_bias_in, conv_bias),
    ):
        fetch = pltpu.make_async_copy(source, target, sems.at[len(fetches)])
        fetch.start()
        fetches.append(fetch)
    space = lax.axis_index("space")
    section = lax.axis_index("tm")
    chan = lax.axis_index("chan")
    row0 = space * rows_here
    groups = LW * ZC // LANES
    lane = lax.broadcasted_iota(jnp.int32, (groups, LANES), 1)
    group = lax.broadcasted_iota(jnp.int32, (groups, LANES), 0)
    low = lane < LANES // 2

    fetches[0].wait()
    chunks[0] = own
    for chunk, (back, turn) in zip(chunks, plan):
        count = chunk.shape[0]
        start = early_in // FS * FS * height - back * FS * height
        if turn is not None:
            blocks = FS * height // count
            start = start + lax.rem(space + (blocks - turn), blocks) * count
        values = chunk[...].astype(jnp.float32)
        for at in range(groups):
            rows[pl.ds(start, count), at, :] = values[:, at * LANES : (at + 1) * LANES]
    for fetch in fetches[1:]:
        fetch.wait()
    mine, other = row_of(own_bias), row_of(other_bias)
    bias = jnp.concatenate(
        [jnp.where(chan == 0, mine, other), jnp.where(chan == 0, other, mine)], axis=1
    )
    lead = early_one - early_two
    frames_one = FS + early_one
    frames_two = FS + early_two

    def run(base, rows_one):
        rows_two = rows_one - 2
        lane_wide = lax.broadcasted_iota(jnp.int32, (rows_one, LW, LANES), 2)

        for frame in range(FS + early_in):
            frame_ok = section * FS - early_in + frame >= 0
            for row in range(rows_one + 2):
                row_abs = row0 - 4 + base + row
                ok = frame_ok & (row_abs >= 0) & (row_abs < height)
                at = frame * height + jnp.clip(row_abs, 0, height - 1)
                here = jnp.where(ok, rows[at], 0.0)
                before = jnp.where(group == 0, 0.0, pltpu.roll(here, 1, 0))
                after = jnp.where(group == groups - 1, 0.0, pltpu.roll(here, groups - 1, 0))
                for col in range(8):
                    source = here
                    if col == 0:
                        source = jnp.where(lane >= LANES - ZC, before, here)
                    if col == 7:
                        source = jnp.where(lane < ZC, after, here)
                    shift = (-ZC * (col - 1)) % LANES
                    one = source if shift == 0 else pltpu.roll(source, shift, 1)
                    two = pltpu.roll(source, (shift + LANES // 2) % LANES, 1)
                    place = window.at[frame, row]
                    place[pl.ds(col, groups, stride=8), :] = jnp.where(low, one, two)

        def input_conv(frame):
            slots = []
            for depth_at in (2, 1, 0):
                source = frame - early_one - 2 + depth_at + early_in
                if source >= 0:
                    slots += [(source, row_at) for row_at in range(3)]
            pieces = []
            for pair in range(0, len(slots), 2):
                source, row_at = slots[pair]
                value = window[source, row_at : row_at + rows_one]
                second_slot = 0.0
                if pair + 1 < len(slots):
                    source, row_at = slots[pair + 1]
                    second_slot = window[source, row_at : row_at + rows_one]
                value = jnp.where(lane_wide < LANES // 2, value, second_slot)
                pieces.append(value.astype(jnp.bfloat16).reshape(rows_one * LW, LANES))
            lhs = jnp.concatenate(pieces, axis=-1)
            pre[frame % 2, 0 : rows_one * LW] = jnp.dot(
                lhs, win[0 : lhs.shape[1]], preferred_element_type=jnp.float32
            )

        def activate(frame, row):
            frame_ok = section * FS - early_one + frame >= 0
            out = pre[frame % 2, row * LW : (row + 1) * LW] + bias
            out = out.astype(jnp.bfloat16).astype(jnp.float32)
            if frame >= early_one:
                mine = jnp.where(
                    chan == 0, out[:, :WIDE], pltpu.roll(out[:, LANES:], C // 2, 1)
                )
                residual[frame - early_one, base + row] = mine.astype(jnp.bfloat16)
            keep = kept(frame_ok, row0 - 3 + base + row, height)
            act = activated(out, row_of(gain) * 0.5, keep)
            acts[frame, base + row] = act.astype(jnp.bfloat16)

        for frame in range(lead + 1):
            input_conv(frame)
            for row in range(rows_one):
                activate(frame, row)
        for frame in range(frames_two - 1):
            later = frame + lead + 1
            row = 0
            input_conv(later)
            for col in range(3):
                first_conv(acts, weight, parts.at[frame % 2], frame, lead, base, rows_two, col)
                while row * 3 < rows_one * (col + 1):
                    activate(later, row)
                    row += 1
            first_finish(parts.at[frame % 2], conv_bias, second.at[frame], base, rows_two)

    by_place(run, rows_here + 6, 2)


def by_place(run, rows, margin):
    count = lax.axis_size("space")
    if count < 2:
        run(0, rows)
        return
    space = lax.axis_index("space")
    outer = (space == 0) | (space == count - 1)

    @pl.when(outer)
    def _():
        run(jnp.where(space == 0, margin, 0), rows - margin)

    @pl.when(jnp.logical_not(outer))
    def _():
        run(0, rows)


def first_conv(acts, weight, parts, frame, lead, base, rows, col):
    places = []
    for depth_at in (2, 1, 0):
        if frame - 2 + depth_at + lead >= 0:
            places += [(depth_at, row_at) for row_at in range(3)]

    def piece(place):
        depth_at, row_at = place
        source = frame - 2 + depth_at + lead
        return acts[source, pl.ds(base + row_at, rows)].reshape(rows * LW, C)

    parts[col, 0 : rows * LW, 0 : C // 2] = conv_part(piece, weight, places, col)


def first_finish(parts, conv_bias, second, base, rows):
    chan = lax.axis_index("chan")
    for row in range(rows):
        total = columns_summed(parts, pl.ds(row * LW, LW))
        total = packed(total + wide_of(conv_bias), chan)
        second[base + row] = total.astype(jnp.bfloat16)
    blank_skipped(second, rows)


def blank_skipped(target, rows):
    skipped = target.shape[0] - rows
    if skipped:
        start = jnp.where(lax.axis_index("space") == 0, 0, rows)
        target[pl.ds(start, skipped)] = jnp.zeros((skipped,) + target.shape[1:], target.dtype)


def first_last(dims, acts, weight, conv_bias, second, parts):
    frame, lead = dims

    def run(base, rows):
        for col in range(3):
            first_conv(acts, weight, parts, frame, lead, base, rows, col)
        first_finish(parts, conv_bias, second, base, rows)

    by_place(run, second.shape[0], 2)


def second_activate(dims, own, other, gain, acts, start, base, rows):
    rows_here, height, early_two = dims
    section = lax.axis_index("tm")
    chan = lax.axis_index("chan")
    row0 = lax.axis_index("space") * rows_here
    half_gain = row_of(gain) * 0.5
    for frame in range(acts.shape[0]):
        frame_ok = section * FS - early_two + start + frame >= 0
        for row in range(rows):
            values = halves(own[frame, base + row], other[frame, base + row], chan)
            keep = kept(frame_ok, row0 - 2 + base + row, height)
            act = activated(values, half_gain, keep)
            acts[frame, base + row] = act.astype(jnp.bfloat16)


def second_lead(dims, own, other, gain, acts):
    def run(base, rows):
        second_activate(dims, own, other, gain, acts, 0, base, rows)

    by_place(run, acts.shape[1], 1)


def second_stage(
    dims, own, other, led, residual, gain, weight, conv_bias, block, acts, parts
):
    early_two = dims[2]
    chan = lax.axis_index("chan")
    ahead = led.shape[0]

    def run(base, rows_two):
        rows = rows_two - 2

        def frame_of(frame, row_at):
            ref, at = (led, frame) if frame < ahead else (acts, frame - ahead)
            return ref[at, pl.ds(base + row_at, rows)].reshape(rows * LW, C)

        def piece(place):
            depth_at, row_at = place
            frames = []
            for frame in range(FS):
                source = frame - 2 + depth_at + early_two
                if source >= 0:
                    frames.append(frame_of(source, row_at))
                else:
                    frames.append(jnp.zeros((rows * LW, C), jnp.bfloat16))
            return jnp.concatenate(frames, axis=0)

        used = (slice(0, FS * rows * LW), slice(0, C // 2))
        taps = [(d, r) for d in (0, 1) for r in range(3) if FS - 3 + d + early_two >= 0]
        for col in range(3):
            if taps:
                parts[(col,) + used] = conv_part(piece, weight, taps, col)
            else:
                parts[col] = jnp.zeros(parts.shape[1:], jnp.float32)
        second_activate(dims, own, other, gain, acts, ahead, base, rows_two)
        for col in range(3):
            taps = [(2, r) for r in range(3)]
            parts[(col,) + used] += conv_part(piece, weight, taps, col)
        for frame in range(FS):
            for row in range(rows):
                total = columns_summed(parts, pl.ds((frame * rows + row) * LW, LW))
                total = total + wide_of(conv_bias)
                total = total + residual[frame, base + row + 2].astype(jnp.float32)
                block[frame, base + row] = packed(total, chan).astype(jnp.bfloat16)
            blank_skipped(block.at[frame], rows)

    by_place(run, led.shape[1], 1)


def third_stage(dims, own, other, weight, up_bias, decoded, acts, raw):
    rows_here, height = dims
    chan = lax.axis_index("chan")
    row0 = lax.axis_index("space") * rows_here
    rows_three = rows_here + 2
    out_chan = weight.shape[1] // 4
    for frame in range(FS):
        for row in range(rows_three):
            values = halves(own[frame, row], other[frame, row], chan)
            values = values * kept(True, row0 - 1 + row, height)
            acts[frame, row] = values.astype(jnp.bfloat16)
    count = FS * rows_here * LW
    source = lax.broadcasted_iota(jnp.int32, (4 * LW, 4 * LW), 0)
    target = lax.broadcasted_iota(jnp.int32, (4 * LW, 4 * LW), 1)
    phase = source // (2 * LW)
    place = source % (2 * LW)
    wanted = (place // LW) * (2 * LW) + (place % LW) * 2 + phase
    shuffle = jnp.where(wanted == target, 1.0, 0.0).astype(jnp.bfloat16)
    column_bias = row_of(up_bias).T
    column = lax.broadcasted_iota(jnp.int32, (out_chan, 2 * LW), 1) % LW
    for row_phase in range(2):
        lhs = [
            acts[:, at : at + rows_here].reshape(count, C)
            for at in (row_phase, row_phase + 1)
        ]
        raw[row_phase] = lax.dot_general(
            weight[row_phase],
            jnp.concatenate(lhs, axis=1),
            (((1,), (1,)), ((), ())),
            preferred_element_type=jnp.float32,
        )
        pairs = []
        for start in range(0, count, 2 * LW):
            left, even, odd, right = (
                raw[row_phase, at * out_chan : (at + 1) * out_chan, start : start + 2 * LW]
                for at in range(4)
            )
            left = jnp.where(column == 0, 0.0, pltpu.roll(left, 1, 1))
            right = jnp.where(column == LW - 1, 0.0, pltpu.roll(right, 2 * LW - 1, 1))
            pair = jnp.concatenate([left + even + column_bias, odd + right + column_bias], axis=1)
            pairs.append(pair.astype(jnp.bfloat16))
        pixels = jnp.dot(
            jnp.concatenate(pairs, axis=0), shuffle, preferred_element_type=jnp.float32
        ).astype(jnp.bfloat16)
        for at in range(len(pairs)):
            frame, row = divmod(2 * at, rows_here)
            part = pixels[at * out_chan : (at + 1) * out_chan]
            decoded[frame, 2 * row + row_phase] = part[:, : 2 * LW]
            decoded[frame, 2 * row + 2 + row_phase] = part[:, 2 * LW :]


def prepare(own_in, other_in, up_in, first_in, win, phases, first, own, up, sems):
    fetches = []
    for source, target in ((own_in, own), (up_in, up), (first_in, first)):
        fetch = pltpu.make_async_copy(source, target, sems.at[len(fetches)])
        fetch.start()
        fetches.append(fetch)
    chan = lax.axis_index("chan")
    fetches[0].wait()
    mine, other = own[...].astype(jnp.float32), other_in[...].astype(jnp.float32)
    low = jnp.where(chan == 0, mine, other)
    high = jnp.where(chan == 0, other, mine)
    joint = jnp.concatenate([low, high], axis=0).T.astype(jnp.bfloat16)
    blank = jnp.zeros((LANES // 2, C), jnp.bfloat16)
    for slot in range(10):
        win[slot * 64 : slot * 64 + 64, :] = blank
    for slot in range(9):
        source = ((2 - slot // 3) * 3 + slot % 3) * 3 * ZC
        win[slot * 64 : slot * 64 + 3 * ZC, :] = joint[source : source + 3 * ZC]
    fetches[1].wait()
    count = up.shape[1]
    for row_phase, split in enumerate((((0,), (1, 2)), ((0, 1), (2,)))):
        for row_at, taps in enumerate(split):
            cols = []
            for c in range(3):
                cut = pl.ds(c * C, C)
                value = up[taps[0], :, cut].astype(jnp.float32)
                for tap in taps[1:]:
                    value = value + up[tap, :, cut].astype(jnp.float32)
                cols.append(value)
            grouped = (cols[0], cols[1] + cols[2], cols[0] + cols[1], cols[2])
            for at, value in enumerate(grouped):
                target = (row_phase, pl.ds(at * count, count), pl.ds(row_at * C, C))
                phases[target] = value.astype(jnp.bfloat16)
    fetches[2].wait()


def limits(mib):
    return pltpu.CompilerParams(vmem_limit_bytes=mib * 1024 * 1024)


def cost(tap_rows):
    return pl.CostEstimate(
        flops=2 * tap_rows * 3 * C * WIDE, bytes_accessed=8 * tap_rows * C, transcendentals=0
    )


def shards(
    latent,
    in_weight,
    in_bias,
    first_gain,
    first_weight,
    first_bias,
    second_gain,
    second_weight,
    second_bias,
    up_weight,
    up_bias,
):
    space_count = lax.axis_size("space")
    tm_count = lax.axis_size("tm")
    rows_here = latent.shape[1] // FS
    height = rows_here * space_count
    groups = LW * ZC // LANES
    earlier = FS * (tm_count - 1)
    early_two, early_one, early_in = min(2, earlier), min(4, earlier), min(6, earlier)
    swap = [(0, 1), (1, 0)]

    plan = []
    if space_count <= 4:
        section_chunks = [latent[0]]
        for turn in range(1, space_count):
            pairs = [(i, (i + turn) % space_count) for i in range(space_count)]
            section_chunks.append(lax.ppermute(latent[0], "space", pairs))
        turns = list(range(space_count))
    else:
        section_chunks = [lax.all_gather(latent[0], "space", axis=0, tiled=True)]
        turns = [None]
    chunks = list(section_chunks)
    plan = [(0, turn) for turn in turns]
    for back in range(1, early_in // FS + 1):
        pairs = [(i, (i + back) % tm_count) for i in range(tm_count)]
        for chunk, turn in zip(section_chunks, turns):
            chunks.append(lax.ppermute(chunk, "tm", pairs))
            plan.append((back, turn))

    stored_in = jnp.swapaxes(in_weight, 0, 1)
    stored_up = jnp.swapaxes(up_weight, 1, 2)
    out_chan = up_weight.shape[-1]
    def stay(array):
        return pltpu.with_memory_space_constraint(array, pltpu.HBM)

    vmem, hbm = pl.BlockSpec(memory_space=pltpu.VMEM), pl.BlockSpec(memory_space=pltpu.HBM)
    stored_first = jnp.swapaxes(first_weight, 1, 2)
    win, phases, fetched_first = pl.pallas_call(
        prepare,
        out_shape=(
            jax.ShapeDtypeStruct((5 * LANES, C), jnp.bfloat16),
            jax.ShapeDtypeStruct((2, 4 * out_chan, 2 * C), jnp.bfloat16),
            jax.ShapeDtypeStruct(stored_first.shape, jnp.bfloat16),
        ),
        in_specs=[hbm, vmem, hbm, hbm],
        out_specs=(vmem,) * 3,
        scratch_shapes=[
            pltpu.VMEM(stored_in.shape, jnp.bfloat16),
            pltpu.VMEM(stored_up.shape, jnp.bfloat16),
            pltpu.SemaphoreType.DMA((3,)),
        ],
        compiler_params=limits(14),
        name="prepare",
    )(
        stay(stored_in),
        lax.ppermute(stored_in, "chan", swap),
        stay(stored_up),
        stay(stored_first),
    )

    rows_two = rows_here + 4
    frames_two = FS + early_two
    ahead = frames_two - 1
    block_shape = (FS, rows_here + 2, LW, WIDE)
    acts_one = (FS + early_one, rows_here + 6, LW, C)
    early = (early_in, early_one, early_two)
    own_lead, residual, acts = pl.pallas_call(
        functools.partial(first_stage, (rows_here, height, early, tuple(plan))),
        out_shape=(
            jax.ShapeDtypeStruct((ahead, rows_two, LW, WIDE), jnp.bfloat16),
            jax.ShapeDtypeStruct((FS, rows_here + 6, LW, WIDE), jnp.bfloat16),
            jax.ShapeDtypeStruct(acts_one, jnp.bfloat16),
        ),
        in_specs=[hbm] + [vmem] * (len(chunks) + 2) + [hbm] * 3,
        out_specs=(vmem,) * 3,
        scratch_shapes=[
            pltpu.VMEM(((FS + early_in) * height, groups, LANES), jnp.float32),
            pltpu.VMEM((FS + early_in, rows_here + 8, LW, LANES), jnp.float32),
            pltpu.VMEM((2, (rows_here + 6) * LW, C), jnp.float32),
            pltpu.VMEM((2, 3, rows_two * LW, WIDE), jnp.float32),
            pltpu.VMEM(chunks[0].shape, jnp.bfloat16),
            pltpu.VMEM(in_bias.shape, jnp.float32),
            pltpu.VMEM(first_gain.shape, jnp.float32),
            pltpu.VMEM(first_bias.shape, jnp.float32),
            pltpu.SemaphoreType.DMA((4,)),
        ],
        compiler_params=limits(20),
        name="first_stage",
    )(
        stay(chunks[0]),
        *chunks[1:],
        win,
        lax.ppermute(in_bias, "chan", swap),
        fetched_first,
        stay(in_bias),
        stay(first_gain),
        stay(first_bias),
    )
    other_lead = lax.ppermute(own_lead, "chan", swap)
    own_last = pl.pallas_call(
        functools.partial(first_last, (ahead, early_one - early_two)),
        out_shape=jax.ShapeDtypeStruct((rows_two, LW, WIDE), jnp.bfloat16),
        in_specs=[vmem] * 3,
        out_specs=vmem,
        scratch_shapes=[pltpu.VMEM((3, rows_two * LW, WIDE), jnp.float32)],
        compiler_params=limits(8),
        name="first_last",
        cost_estimate=cost(9 * rows_two * LW),
    )(acts, fetched_first, first_bias)
    other_last = lax.ppermute(own_last, "chan", swap)

    dims = (rows_here, height, early_two)
    led = pl.pallas_call(
        functools.partial(second_lead, dims),
        out_shape=jax.ShapeDtypeStruct((ahead, rows_two, LW, C), jnp.bfloat16),
        in_specs=[vmem] * 3,
        out_specs=vmem,
        compiler_params=limits(8),
        name="second_lead",
        cost_estimate=cost(2 * rows_two * LW),
    )(own_lead, other_lead, second_gain)
    block_own = pl.pallas_call(
        functools.partial(second_stage, dims),
        out_shape=jax.ShapeDtypeStruct(block_shape, jnp.bfloat16),
        in_specs=[vmem] * 7,
        out_specs=vmem,
        scratch_shapes=[
            pltpu.VMEM((1, rows_two, LW, C), jnp.bfloat16),
            pltpu.VMEM((3, FS * (rows_here + 2) * LW, WIDE), jnp.float32),
        ],
        compiler_params=limits(12),
        name="second_stage",
    )(
        own_last[None],
        other_last[None],
        led,
        residual,
        second_gain,
        jnp.swapaxes(second_weight, 1, 2),
        second_bias,
    )
    block_other = lax.ppermute(block_own, "chan", swap)

    return pl.pallas_call(
        functools.partial(third_stage, (rows_here, height)),
        out_shape=jax.ShapeDtypeStruct((FS, 2 * rows_here, out_chan, 2 * LW), jnp.bfloat16),
        in_specs=[vmem] * 4,
        out_specs=vmem,
        scratch_shapes=[
            pltpu.VMEM((FS, rows_here + 2, LW, C), jnp.bfloat16),
            pltpu.VMEM((2, 4 * out_chan, FS * rows_here * LW), jnp.float32),
        ],
        compiler_params=limits(12),
        name="third_stage",
    )(block_own, block_other, phases, up_bias)


def solution(mesh):
    placed = (
        P(("groups", "tm"), "space", None),
        P(None, "chan"),
        P("chan"),
        P(),
        P(None, None, "chan"),
        P("chan"),
        P(),
        P(None, None, "chan"),
        P("chan"),
        P(None, None, "chan"),
        P("chan"),
    )
    return jax.shard_map(
        shards,
        mesh=mesh,
        in_specs=placed,
        out_specs=P(("groups", "tm"), "space", "chan", None),
        check_vma=False,
    )
```

```python
import functools

import jax
import jax.numpy as jnp
from jax import lax
from jax.experimental import pallas as pl
from jax.experimental.pallas import tpu as pltpu
from jax.sharding import PartitionSpec as P

ZC = 16
C = 384
FS = 2
LW = 64
LANES = 128
WIDE = 256

epsilon = 1e-06


def row_of(vector):
    return vector[...].reshape(1, vector.shape[0])


def wide_of(vector):
    row = row_of(vector)
    return jnp.concatenate([row, jnp.zeros((1, WIDE - C // 2), row.dtype)], axis=-1)


def activated(values, gain_half, keep):
    squares = jnp.sum(values * values, axis=-1, keepdims=True)
    factor = lax.rsqrt(squares * (1.0 / C) + epsilon) * keep
    half = values * factor * gain_half
    return half + half * jnp.tanh(half)


def kept(frame_ok, row, height):
    return jnp.where(frame_ok & (row >= 0) & (row < height), 1.0, 0.0)


def joined(low, high):
    lane = lax.broadcasted_iota(jnp.int32, (low.shape[0], LANES), 1)
    middle = jnp.where(lane < LANES // 2, low[:, LANES:], high[:, :LANES])
    return jnp.concatenate([low[:, :LANES], middle, high[:, LANES:]], axis=-1)


def packed(half, chan):
    return jnp.where(chan == 0, half, pltpu.roll(half, WIDE - C // 2, 1))


def halves(own, other, chan):
    low = jnp.where(chan == 0, own, other)
    high = jnp.where(chan == 0, other, own)
    return joined(low.astype(jnp.float32), high.astype(jnp.float32))


def conv_part(piece, weight, places, col):
    lhs = [piece(place) for place in places]
    cut = slice(col * C, (col + 1) * C)
    rhs = [weight[depth_at * 3 + row_at, :, cut] for depth_at, row_at in places]
    return lax.dot_general(
        jnp.concatenate(lhs, axis=1),
        jnp.concatenate(rhs, axis=1),
        (((1,), (1,)), ((), ())),
        preferred_element_type=jnp.float32,
    )


def columns_summed(parts, span):
    left, here, right = (parts[col, span, :] for col in range(3))
    group = lax.broadcasted_iota(jnp.int32, (8, WIDE), 0)
    wrapped = jnp.where(group == 0, 0.0, pltpu.roll(left[LW - 8 :], 1, 0))
    left = jnp.concatenate([wrapped, left[: LW - 8]], axis=0)
    wrapped = jnp.where(group == 7, 0.0, pltpu.roll(right[:8], 7, 0))
    right = jnp.concatenate([right[8:], wrapped], axis=0)
    return left + here + right


def first_stage(dims, *refs):
    rows_here, height, early, plan = dims
    early_in, early_one, early_two = early
    chunks, refs = list(refs[: len(plan)]), refs[len(plan) :]
    win, other_bias, weight, own_bias_in, gain_in, conv_bias_in, *refs = refs
    second, residual, acts, rows, window, pre, parts, *refs = refs
    own, own_bias, gain, conv_bias, sems = refs
    fetches = []
    for source, target in (
        (chunks[0], own),
        (own_bias_in, own_bias),
        (gain_in, gain),
        (conv_bias_in, conv_bias),
    ):
        fetch = pltpu.make_async_copy(source, target, sems.at[len(fetches)])
        fetch.start()
        fetches.append(fetch)
    space = lax.axis_index("space")
    section = lax.axis_index("tm")
    chan = lax.axis_index("chan")
    row0 = space * rows_here
    groups = LW * ZC // LANES
    lane = lax.broadcasted_iota(jnp.int32, (groups, LANES), 1)
    group = lax.broadcasted_iota(jnp.int32, (groups, LANES), 0)
    low = lane < LANES // 2

    fetches[0].wait()
    chunks[0] = own
    for chunk, (back, turn) in zip(chunks, plan):
        count = chunk.shape[0]
        start = early_in // FS * FS * height - back * FS * height
        if turn is not None:
            blocks = FS * height // count
            start = start + lax.rem(space + (blocks - turn), blocks) * count
        values = chunk[...].astype(jnp.float32)
        for at in range(groups):
            rows[pl.ds(start, count), at, :] = values[:, at * LANES : (at + 1) * LANES]
    for fetch in fetches[1:]:
        fetch.wait()
    mine, other = row_of(own_bias), row_of(other_bias)
    bias = jnp.concatenate(
        [jnp.where(chan == 0, mine, other), jnp.where(chan == 0, other, mine)], axis=1
    )
    lead = early_one - early_two
    frames_one = FS + early_one
    frames_two = FS + early_two

    def run(base, rows_one):
        rows_two = rows_one - 2
        lane_wide = lax.broadcasted_iota(jnp.int32, (rows_one, LW, LANES), 2)

        for frame in range(FS + early_in):
            frame_ok = section * FS - early_in + frame >= 0
            for row in range(rows_one + 2):
                row_abs = row0 - 4 + base + row
                ok = frame_ok & (row_abs >= 0) & (row_abs < height)
                at = frame * height + jnp.clip(row_abs, 0, height - 1)
                here = jnp.where(ok, rows[at], 0.0)
                before = jnp.where(group == 0, 0.0, pltpu.roll(here, 1, 0))
                after = jnp.where(group == groups - 1, 0.0, pltpu.roll(here, groups - 1, 0))
                for col in range(8):
                    source = here
                    if col == 0:
                        source = jnp.where(lane >= LANES - ZC, before, here)
                    if col == 7:
                        source = jnp.where(lane < ZC, after, here)
                    shift = (-ZC * (col - 1)) % LANES
                    one = source if shift == 0 else pltpu.roll(source, shift, 1)
                    two = pltpu.roll(source, (shift + LANES // 2) % LANES, 1)
                    window[frame, row, col * 8 : col * 8 + 8, :] = jnp.where(low, one, two)

        def input_conv(frame):
            slots = []
            for depth_at in (2, 1, 0):
                source = frame - early_one - 2 + depth_at + early_in
                if source >= 0:
                    slots += [(source, row_at) for row_at in range(3)]
            pieces = []
            for pair in range(0, len(slots), 2):
                source, row_at = slots[pair]
                value = window[source, row_at : row_at + rows_one]
                second_slot = 0.0
                if pair + 1 < len(slots):
                    source, row_at = slots[pair + 1]
                    second_slot = window[source, row_at : row_at + rows_one]
                value = jnp.where(lane_wide < LANES // 2, value, second_slot)
                pieces.append(value.astype(jnp.bfloat16).reshape(rows_one * LW, LANES))
            lhs = jnp.concatenate(pieces, axis=-1)
            pre[frame % 2, 0 : rows_one * LW] = jnp.dot(
                lhs, win[0 : lhs.shape[1]], preferred_element_type=jnp.float32
            )

        def activate(frame, row):
            frame_ok = section * FS - early_one + frame >= 0
            out = pre[frame % 2, row * LW : (row + 1) * LW] + bias
            out = out.astype(jnp.bfloat16).astype(jnp.float32)
            if frame >= early_one:
                mine = jnp.where(
                    chan == 0, out[:, :WIDE], pltpu.roll(out[:, LANES:], C // 2, 1)
                )
                residual[frame - early_one, base + row] = mine.astype(jnp.bfloat16)
            keep = kept(frame_ok, row0 - 3 + base + row, height)
            act = activated(out, row_of(gain) * 0.5, keep)
            acts[frame, base + row] = act.astype(jnp.bfloat16)

        for frame in range(lead + 1):
            input_conv(frame)
            for row in range(rows_one):
                activate(frame, row)
        for frame in range(frames_two - 1):
            later = frame + lead + 1
            row = 0
            input_conv(later)
            for col in range(3):
                first_conv(acts, weight, parts.at[frame % 2], frame, lead, base, rows_two, col)
                while row * 3 < rows_one * (col + 1):
                    activate(later, row)
                    row += 1
            first_finish(parts.at[frame % 2], conv_bias, second.at[frame], base, rows_two)

    by_place(run, rows_here + 6, 2)


def by_place(run, rows, margin):
    count = lax.axis_size("space")
    if count < 2:
        run(0, rows)
        return
    space = lax.axis_index("space")
    outer = (space == 0) | (space == count - 1)

    @pl.when(outer)
    def _():
        run(jnp.where(space == 0, margin, 0), rows - margin)

    @pl.when(jnp.logical_not(outer))
    def _():
        run(0, rows)


def first_conv(acts, weight, parts, frame, lead, base, rows, col):
    places = []
    for depth_at in (2, 1, 0):
        if frame - 2 + depth_at + lead >= 0:
            places += [(depth_at, row_at) for row_at in range(3)]

    def piece(place):
        depth_at, row_at = place
        source = frame - 2 + depth_at + lead
        return acts[source, pl.ds(base + row_at, rows)].reshape(rows * LW, C)

    parts[col, 0 : rows * LW, 0 : C // 2] = conv_part(piece, weight, places, col)


def first_finish(parts, conv_bias, second, base, rows):
    chan = lax.axis_index("chan")
    for row in range(rows):
        total = columns_summed(parts, pl.ds(row * LW, LW))
        total = packed(total + wide_of(conv_bias), chan)
        second[base + row] = total.astype(jnp.bfloat16)
    blank_skipped(second, rows)


def blank_skipped(target, rows):
    skipped = target.shape[0] - rows
    if skipped:
        start = jnp.where(lax.axis_index("space") == 0, 0, rows)
        target[pl.ds(start, skipped)] = jnp.zeros((skipped,) + target.shape[1:], target.dtype)


def first_last(dims, acts, weight, conv_bias, second, parts):
    frame, lead = dims

    def run(base, rows):
        for col in range(3):
            first_conv(acts, weight, parts, frame, lead, base, rows, col)
        first_finish(parts, conv_bias, second, base, rows)

    by_place(run, second.shape[0], 2)


def second_activate(dims, own, other, gain, acts, start, base, rows):
    rows_here, height, early_two = dims
    section = lax.axis_index("tm")
    chan = lax.axis_index("chan")
    row0 = lax.axis_index("space") * rows_here
    half_gain = row_of(gain) * 0.5
    for frame in range(acts.shape[0]):
        frame_ok = section * FS - early_two + start + frame >= 0
        for row in range(rows):
            values = halves(own[frame, base + row], other[frame, base + row], chan)
            keep = kept(frame_ok, row0 - 2 + base + row, height)
            act = activated(values, half_gain, keep)
            acts[frame, base + row] = act.astype(jnp.bfloat16)


def second_lead(dims, own, other, gain, acts):
    def run(base, rows):
        second_activate(dims, own, other, gain, acts, 0, base, rows)

    by_place(run, acts.shape[1], 1)


def second_stage(
    dims, own, other, led, residual, gain, weight, conv_bias, block, acts, parts
):
    early_two = dims[2]
    chan = lax.axis_index("chan")
    ahead = led.shape[0]

    def run(base, rows_two):
        rows = rows_two - 2

        def frame_of(frame, row_at):
            ref, at = (led, frame) if frame < ahead else (acts, frame - ahead)
            return ref[at, pl.ds(base + row_at, rows)].reshape(rows * LW, C)

        def piece(place):
            depth_at, row_at = place
            frames = []
            for frame in range(FS):
                source = frame - 2 + depth_at + early_two
                if source >= 0:
                    frames.append(frame_of(source, row_at))
                else:
                    frames.append(jnp.zeros((rows * LW, C), jnp.bfloat16))
            return jnp.concatenate(frames, axis=0)

        used = (slice(0, FS * rows * LW), slice(0, C // 2))
        taps = [(d, r) for d in (0, 1) for r in range(3) if FS - 3 + d + early_two >= 0]
        for col in range(3):
            if taps:
                parts[(col,) + used] = conv_part(piece, weight, taps, col)
            else:
                parts[col] = jnp.zeros(parts.shape[1:], jnp.float32)
        second_activate(dims, own, other, gain, acts, ahead, base, rows_two)
        for col in range(3):
            taps = [(2, r) for r in range(3)]
            parts[(col,) + used] += conv_part(piece, weight, taps, col)
        for frame in range(FS):
            for row in range(rows):
                total = columns_summed(parts, pl.ds((frame * rows + row) * LW, LW))
                total = total + wide_of(conv_bias)
                total = total + residual[frame, base + row + 2].astype(jnp.float32)
                block[frame, base + row] = packed(total, chan).astype(jnp.bfloat16)
            blank_skipped(block.at[frame], rows)

    by_place(run, led.shape[1], 1)


def third_stage(dims, own, other, weight, up_bias, decoded, acts, raw):
    rows_here, height = dims
    chan = lax.axis_index("chan")
    row0 = lax.axis_index("space") * rows_here
    rows_three = rows_here + 2
    out_chan = weight.shape[1] // 4
    for frame in range(FS):
        for row in range(rows_three):
            values = halves(own[frame, row], other[frame, row], chan)
            values = values * kept(True, row0 - 1 + row, height)
            acts[frame, row] = values.astype(jnp.bfloat16)
    count = FS * rows_here * LW
    source = lax.broadcasted_iota(jnp.int32, (4 * LW, 4 * LW), 0)
    target = lax.broadcasted_iota(jnp.int32, (4 * LW, 4 * LW), 1)
    phase = source // (2 * LW)
    place = source % (2 * LW)
    column = place % 8 * 8 + place % LW // 8
    wanted = (place // LW) * (2 * LW) + column * 2 + phase
    shuffle = jnp.where(wanted == target, 1.0, 0.0).astype(jnp.bfloat16)
    column_bias = row_of(up_bias).T
    place = lax.broadcasted_iota(jnp.int32, (out_chan, 2 * LW), 1) % LW
    for row_phase in range(2):
        lhs = [
            acts[:, at : at + rows_here].reshape(count, C)
            for at in (row_phase, row_phase + 1)
        ]
        raw[row_phase] = lax.dot_general(
            weight[row_phase],
            jnp.concatenate(lhs, axis=1),
            (((1,), (1,)), ((), ())),
            preferred_element_type=jnp.float32,
        )
    pairs, targets = [], []
    for row_phase in range(2):
        for start in range(0, count, 2 * LW):
            left, even, odd, right = (
                raw[row_phase, at * out_chan : (at + 1) * out_chan, start : start + 2 * LW]
                for at in range(4)
            )
            wrapped = jnp.where(place == 0, 0.0, pltpu.roll(left, 2 * LW - (LW - 9), 1))
            left = jnp.where(place < 8, wrapped, pltpu.roll(left, 8, 1))
            wrapped = jnp.where(place == LW - 1, 0.0, pltpu.roll(right, LW - 9, 1))
            right = jnp.where(place >= LW - 8, wrapped, pltpu.roll(right, 2 * LW - 8, 1))
            pair = jnp.concatenate([left + even + column_bias, odd + right + column_bias], axis=1)
            pairs.append(pair.astype(jnp.bfloat16))
            frame, row = divmod(start // LW, rows_here)
            targets.append((frame, 2 * row + row_phase))
    pixels = jnp.dot(
        jnp.concatenate(pairs, axis=0), shuffle, preferred_element_type=jnp.float32
    ).astype(jnp.bfloat16)
    for at, (frame, row) in enumerate(targets):
        part = pixels[at * out_chan : (at + 1) * out_chan]
        decoded[frame, row] = part[:, : 2 * LW]
        decoded[frame, row + 2] = part[:, 2 * LW :]


def prepare(own_in, other_in, up_in, first_in, win, phases, first, own, up, sems):
    fetches = []
    for source, target in ((own_in, own), (up_in, up), (first_in, first)):
        fetch = pltpu.make_async_copy(source, target, sems.at[len(fetches)])
        fetch.start()
        fetches.append(fetch)
    chan = lax.axis_index("chan")
    fetches[0].wait()
    mine, other = own[...].astype(jnp.float32), other_in[...].astype(jnp.float32)
    low = jnp.where(chan == 0, mine, other)
    high = jnp.where(chan == 0, other, mine)
    joint = jnp.concatenate([low, high], axis=0).T.astype(jnp.bfloat16)
    blank = jnp.zeros((LANES // 2, C), jnp.bfloat16)
    for slot in range(10):
        win[slot * 64 : slot * 64 + 64, :] = blank
    for slot in range(9):
        source = ((2 - slot // 3) * 3 + slot % 3) * 3 * ZC
        win[slot * 64 : slot * 64 + 3 * ZC, :] = joint[source : source + 3 * ZC]
    fetches[1].wait()
    count = up.shape[1]
    for row_phase, split in enumerate((((0,), (1, 2)), ((0, 1), (2,)))):
        for row_at, taps in enumerate(split):
            cols = []
            for c in range(3):
                cut = pl.ds(c * C, C)
                value = up[taps[0], :, cut].astype(jnp.float32)
                for tap in taps[1:]:
                    value = value + up[tap, :, cut].astype(jnp.float32)
                cols.append(value)
            grouped = (cols[0], cols[1] + cols[2], cols[0] + cols[1], cols[2])
            for at, value in enumerate(grouped):
                target = (row_phase, pl.ds(at * count, count), pl.ds(row_at * C, C))
                phases[target] = value.astype(jnp.bfloat16)
    fetches[2].wait()


def limits(mib):
    return pltpu.CompilerParams(vmem_limit_bytes=mib * 1024 * 1024)


def cost(tap_rows):
    return pl.CostEstimate(
        flops=2 * tap_rows * 3 * C * WIDE, bytes_accessed=8 * tap_rows * C, transcendentals=0
    )


def shards(
    latent,
    in_weight,
    in_bias,
    first_gain,
    first_weight,
    first_bias,
    second_gain,
    second_weight,
    second_bias,
    up_weight,
    up_bias,
):
    space_count = lax.axis_size("space")
    tm_count = lax.axis_size("tm")
    rows_here = latent.shape[1] // FS
    height = rows_here * space_count
    groups = LW * ZC // LANES
    earlier = FS * (tm_count - 1)
    early_two, early_one, early_in = min(2, earlier), min(4, earlier), min(6, earlier)
    swap = [(0, 1), (1, 0)]

    plan = []
    if space_count <= 4:
        section_chunks = [latent[0]]
        for turn in range(1, space_count):
            pairs = [(i, (i + turn) % space_count) for i in range(space_count)]
            section_chunks.append(lax.ppermute(latent[0], "space", pairs))
        turns = list(range(space_count))
    else:
        section_chunks = [lax.all_gather(latent[0], "space", axis=0, tiled=True)]
        turns = [None]
    chunks = list(section_chunks)
    plan = [(0, turn) for turn in turns]
    for back in range(1, early_in // FS + 1):
        pairs = [(i, (i + back) % tm_count) for i in range(tm_count)]
        for chunk, turn in zip(section_chunks, turns):
            chunks.append(lax.ppermute(chunk, "tm", pairs))
            plan.append((back, turn))

    stored_in = jnp.swapaxes(in_weight, 0, 1)
    stored_up = jnp.swapaxes(up_weight, 1, 2)
    out_chan = up_weight.shape[-1]
    other_bias = lax.ppermute(in_bias, "chan", swap)
    def stay(array):
        return pltpu.with_memory_space_constraint(array, pltpu.HBM)

    vmem, hbm = pl.BlockSpec(memory_space=pltpu.VMEM), pl.BlockSpec(memory_space=pltpu.HBM)
    stored_first = jnp.swapaxes(first_weight, 1, 2)
    win, phases, fetched_first = pl.pallas_call(
        prepare,
        out_shape=(
            jax.ShapeDtypeStruct((5 * LANES, C), jnp.bfloat16),
            jax.ShapeDtypeStruct((2, 4 * out_chan, 2 * C), jnp.bfloat16),
            jax.ShapeDtypeStruct(stored_first.shape, jnp.bfloat16),
        ),
        in_specs=[hbm, vmem, hbm, hbm],
        out_specs=(vmem,) * 3,
        scratch_shapes=[
            pltpu.VMEM(stored_in.shape, jnp.bfloat16),
            pltpu.VMEM(stored_up.shape, jnp.bfloat16),
            pltpu.SemaphoreType.DMA((3,)),
        ],
        compiler_params=limits(14),
        name="prepare",
    )(
        stay(stored_in),
        lax.ppermute(stored_in, "chan", swap),
        stay(stored_up),
        stay(stored_first),
    )

    rows_two = rows_here + 4
    frames_two = FS + early_two
    ahead = frames_two - 1
    block_shape = (FS, rows_here + 2, LW, WIDE)
    acts_one = (FS + early_one, rows_here + 6, LW, C)
    early = (early_in, early_one, early_two)
    own_lead, residual, acts = pl.pallas_call(
        functools.partial(first_stage, (rows_here, height, early, tuple(plan))),
        out_shape=(
            jax.ShapeDtypeStruct((ahead, rows_two, LW, WIDE), jnp.bfloat16),
            jax.ShapeDtypeStruct((FS, rows_here + 6, LW, WIDE), jnp.bfloat16),
            jax.ShapeDtypeStruct(acts_one, jnp.bfloat16),
        ),
        in_specs=[hbm] + [vmem] * (len(chunks) + 2) + [hbm] * 3,
        out_specs=(vmem,) * 3,
        scratch_shapes=[
            pltpu.VMEM(((FS + early_in) * height, groups, LANES), jnp.float32),
            pltpu.VMEM((FS + early_in, rows_here + 8, LW, LANES), jnp.float32),
            pltpu.VMEM((2, (rows_here + 6) * LW, C), jnp.float32),
            pltpu.VMEM((2, 3, rows_two * LW, WIDE), jnp.float32),
            pltpu.VMEM(chunks[0].shape, jnp.bfloat16),
            pltpu.VMEM(in_bias.shape, jnp.float32),
            pltpu.VMEM(first_gain.shape, jnp.float32),
            pltpu.VMEM(first_bias.shape, jnp.float32),
            pltpu.SemaphoreType.DMA((4,)),
        ],
        compiler_params=limits(20),
        name="first_stage",
    )(
        stay(chunks[0]),
        *chunks[1:],
        win,
        other_bias,
        fetched_first,
        stay(in_bias),
        stay(first_gain),
        stay(first_bias),
    )
    other_lead = lax.ppermute(own_lead, "chan", swap)
    own_last = pl.pallas_call(
        functools.partial(first_last, (ahead, early_one - early_two)),
        out_shape=jax.ShapeDtypeStruct((rows_two, LW, WIDE), jnp.bfloat16),
        in_specs=[vmem] * 3,
        out_specs=vmem,
        scratch_shapes=[pltpu.VMEM((3, rows_two * LW, WIDE), jnp.float32)],
        compiler_params=limits(8),
        name="first_last",
        cost_estimate=cost(9 * rows_two * LW),
    )(acts, fetched_first, first_bias)
    other_last = lax.ppermute(own_last, "chan", swap)

    dims = (rows_here, height, early_two)
    led = pl.pallas_call(
        functools.partial(second_lead, dims),
        out_shape=jax.ShapeDtypeStruct((ahead, rows_two, LW, C), jnp.bfloat16),
        in_specs=[vmem] * 3,
        out_specs=vmem,
        compiler_params=limits(8),
        name="second_lead",
        cost_estimate=cost(2 * rows_two * LW),
    )(own_lead, other_lead, second_gain)
    block_own = pl.pallas_call(
        functools.partial(second_stage, dims),
        out_shape=jax.ShapeDtypeStruct(block_shape, jnp.bfloat16),
        in_specs=[vmem] * 7,
        out_specs=vmem,
        scratch_shapes=[
            pltpu.VMEM((1, rows_two, LW, C), jnp.bfloat16),
            pltpu.VMEM((3, FS * (rows_here + 2) * LW, WIDE), jnp.float32),
        ],
        compiler_params=limits(12),
        name="second_stage",
    )(
        own_last[None],
        other_last[None],
        led,
        residual,
        second_gain,
        jnp.swapaxes(second_weight, 1, 2),
        second_bias,
    )
    block_other = lax.ppermute(block_own, "chan", swap)

    return pl.pallas_call(
        functools.partial(third_stage, (rows_here, height)),
        out_shape=jax.ShapeDtypeStruct((FS, 2 * rows_here, out_chan, 2 * LW), jnp.bfloat16),
        in_specs=[vmem] * 4,
        out_specs=vmem,
        scratch_shapes=[
            pltpu.VMEM((FS, rows_here + 2, LW, C), jnp.bfloat16),
            pltpu.VMEM((2, 4 * out_chan, FS * rows_here * LW), jnp.float32),
        ],
        compiler_params=limits(12),
        name="third_stage",
    )(block_own, block_other, phases, up_bias)


def solution(mesh):
    placed = (
        P(("groups", "tm"), "space", None),
        P(None, "chan"),
        P("chan"),
        P(),
        P(None, None, "chan"),
        P("chan"),
        P(),
        P(None, None, "chan"),
        P("chan"),
        P(None, None, "chan"),
        P("chan"),
    )
    return jax.shard_map(
        shards,
        mesh=mesh,
        in_specs=placed,
        out_specs=P(("groups", "tm"), "space", "chan", None),
        check_vma=False,
    )
```
